32 devices in a mesh: seq: 4 (over y, x), fsdp: 8 (over z, core).
Axes of the slice: x: 2, y: 2, z: 4, core: 2. Of those that a mesh axis runs over, the one named last changes fastest.
Arguments:
- tokens: bfloat16 [16, 512, 768], P('fsdp', 'seq'), may hold values from -4 to 4
- lengths: int32 [16], P('fsdp'), may hold values from 64 to 512, as said below
- cotangent: bfloat16 [16, 512, 768], P('fsdp', 'seq'), may hold values from -6 to 6
- proj_weight: bfloat16 [768, 2304], P('fsdp'), may hold values from -0.21875 to 0.21875
- qv_bias: bfloat16 [1536], P('fsdp'), may hold values from -3 to 3
- out_weight: bfloat16 [768, 768], P('fsdp'), may hold values from -3.5 to 3.5
- out_bias: bfloat16 [768], P('fsdp'), may hold values from -3 to 3
- norm1_gain: bfloat16 [768], P('fsdp'), may hold values from 0.5 to 1.5
- norm1_bias: bfloat16 [768], P('fsdp'), may hold values from -3 to 3
- up_weight: bfloat16 [768, 3072], P('fsdp'), may hold values from -0.21875 to 0.21875
- up_bias: bfloat16 [3072], P('fsdp'), may hold values from -3 to 3
- down_weight: bfloat16 [3072, 768], P('fsdp'), may hold values from -0.109375 to 0.109375
- down_bias: bfloat16 [768], P('fsdp'), may hold values from -3 to 3
- norm2_gain: bfloat16 [768], P('fsdp'), may hold values from 0.5 to 1.5
- norm2_bias: bfloat16 [768], P('fsdp'), may hold values from -3 to 3
Outputs:
- hidden_out: bfloat16 [16, 512, 768], P('fsdp', 'seq')
- tokens_grad: float32 [16, 512, 768], P('fsdp', 'seq')
- proj_grad: float32 [768, 2304], P('fsdp')
- qv_bias_grad: float32 [1536], P('fsdp')
- out_weight_grad: float32 [768, 768], P('fsdp')
- out_bias_grad: float32 [768], P('fsdp')
- norm1_gain_grad: float32 [768], P('fsdp')
- norm1_bias_grad: float32 [768], P('fsdp')
- up_weight_grad: float32 [768, 3072], P('fsdp')
- up_bias_grad: float32 [3072], P('fsdp')
- down_weight_grad: float32 [3072, 768], P('fsdp')
- down_bias_grad: float32 [768], P('fsdp')
- norm2_gain_grad: float32 [768], P('fsdp')
- norm2_bias_grad: float32 [768], P('fsdp')
The draws below stay inside these ranges and needn't reach their ends.
Inputs may be any that keep to these rules, and one draw needn't show every extreme that they name: Keys at positions lengths[s] and beyond are padding; some sequence has all 512 tokens valid.
All inputs are finite; a program needn't handle non-finite values.
Results may differ from the reference program's by a relative error of at most 0.013.
Values may be sent and summed in bfloat16 or wider, within the bound.
No kernel may reach another device: no remote copies, remote signals or barrier semaphores. Data moves between devices by JAX's collectives and lax.ppermute only.
A program may use at most 128 MiB of HBM per device.

```python
import math
import jax
import jax.numpy as jnp
from jax import lax

D = 768
HEADS = 12
HEAD_DIM = 64
FF = 3072
L = 512
SEQS = 16


def draw_tokens(key, part):
    base_key = jax.random.fold_in(jax.random.fold_in(key, 11), 0)
    values = jnp.clip(jax.random.normal(base_key, (SEQS, L, D), jnp.float32), -4.0, 4.0)
    return values.astype(jnp.bfloat16)


def draw_lengths(key, part):
    first_key, second_key = jax.random.split(jax.random.fold_in(key, 23))
    drawn = jax.random.randint(first_key, (SEQS,), L // 8, L + 1)
    chosen = jax.random.randint(second_key, (), 0, SEQS)
    return jnp.where(jnp.arange(SEQS) == chosen, L, drawn).astype(jnp.int32)


def levels(own_key, extent, shards, least, high):
    loudness = 1.0
    for position, parts in shards:
        draws = jax.random.uniform(jax.random.fold_in(jax.random.fold_in(own_key, 6), position), (parts,), jnp.float32, least / len(shards), high / len(shards))
        loudness = loudness * jnp.repeat(jnp.exp(draws), extent[position] // parts).reshape((-1,) + (1,) * (len(extent) - 1 - position))
    return loudness


def scatter_about(stream_key, extent, deviation, bound, cuts=(), held_as=jnp.bfloat16):
    array = jax.random.normal(stream_key, extent, jnp.float32) * deviation
    if len(cuts) > 0:
        array = levels(stream_key, extent, cuts, -0.22, 0.18) * array
    return jnp.clip(array, min=-bound, max=bound).astype(held_as)


def setup_inputs(seed: int = 0) -> dict:
    key_list = jax.random.split(jax.random.key(seed), 16)
    tokens = draw_tokens(jax.random.fold_in(key_list[15], 71), 0)
    lengths = draw_lengths(jax.random.fold_in(key_list[15], 71), 0)
    cotangent = scatter_about(key_list[2], (SEQS, L, D), 1.0, 6.0, ((0, 8), (1, 4)))
    proj_weight = scatter_about(key_list[3], (D, 3 * D), D ** -0.5, 0.21875, ((0, 8),))
    qv_bias = scatter_about(key_list[4], (2 * D,), 0.5, 3.0, ((0, 8),))
    out_weight = scatter_about(key_list[5], (D, D), (max(D // 256, 1)) ** -0.5, 3.5, ((0, 8),))
    out_bias = scatter_about(key_list[6], (D,), 0.5, 3.0, ((0, 8),))
    norm1_gain = jnp.clip(1.0 + 0.1 * jax.random.normal(key_list[7], (D,), jnp.float32), 0.5, 1.5).astype(jnp.bfloat16)
    norm1_bias = scatter_about(key_list[8], (D,), 0.5, 3.0, ((0, 8),))
    up_weight = scatter_about(key_list[9], (D, FF), D ** -0.5, 0.21875, ((0, 8),))
    up_bias = scatter_about(key_list[10], (FF,), 0.5, 3.0, ((0, 8),))
    down_weight = scatter_about(key_list[11], (FF, D), FF ** -0.5, 0.109375, ((0, 8),))
    down_bias = scatter_about(key_list[12], (D,), 0.5, 3.0, ((0, 8),))
    norm2_gain = jnp.clip(1.0 + 0.1 * jax.random.normal(key_list[13], (D,), jnp.float32), 0.5, 1.5).astype(jnp.bfloat16)
    norm2_bias = scatter_about(key_list[14], (D,), 0.5, 3.0, ((0, 8),))
    return {"tokens": tokens, "lengths": lengths, "cotangent": cotangent, "proj_weight": proj_weight, "qv_bias": qv_bias, "out_weight": out_weight, "out_bias": out_bias, "norm1_gain": norm1_gain, "norm1_bias": norm1_bias, "up_weight": up_weight, "up_bias": up_bias, "down_weight": down_weight, "down_bias": down_bias, "norm2_gain": norm2_gain, "norm2_bias": norm2_bias}


epsilon = 1e-05
masked_score = -1e+30

def rounded(value):
    return lax.optimization_barrier(value.astype(jnp.bfloat16)).astype(jnp.float32)

def normalize(rows):
    centred = rows - lax.optimization_barrier(jnp.mean(rows, axis=-1, keepdims=True))
    inv_scale = lax.rsqrt(lax.optimization_barrier(jnp.mean(centred * centred, axis=-1, keepdims=True)) + epsilon)
    return (centred * inv_scale, inv_scale)

def norm_back(grad_norm, normed, inv_scale):
    first_mean = lax.optimization_barrier(jnp.mean(grad_norm, axis=-1, keepdims=True))
    second_mean = lax.optimization_barrier(jnp.mean(grad_norm * normed, axis=-1, keepdims=True))
    return inv_scale * (grad_norm - first_mean - normed * second_mean)

def gelu_pair(pre_act):
    cumulative = 0.5 * (1.0 + jax.scipy.special.erf(pre_act * (1.0 / math.sqrt(2.0))))
    density = jnp.exp(-0.5 * pre_act * pre_act) * (1.0 / math.sqrt(2.0 * math.pi))
    return (pre_act * cumulative, cumulative + pre_act * density)

def layer_group(params, group_tokens, group_cot, group_lengths):
    proj_weight, qv_bias, out_weight, out_bias, norm1_gain, norm1_bias, up_weight, up_bias, down_weight, down_bias, norm2_gain, norm2_bias = params
    group_size = group_tokens.shape[0]
    row_count = group_size * L
    scale_factor = 1.0 / math.sqrt(HEAD_DIM)
    flat_tokens = group_tokens.reshape(row_count, D)
    qv_float = qv_bias.astype(jnp.float32)
    full_bias = jnp.concatenate([qv_float[:D], jnp.zeros((D,), jnp.float32), qv_float[D:]])
    proj_act = jnp.dot(flat_tokens, proj_weight, preferred_element_type=jnp.float32) + full_bias
    split_proj = rounded(proj_act).reshape(group_size, L, 3, HEADS, HEAD_DIM)
    query_side = split_proj[:, :, 0]
    key_side = split_proj[:, :, 1]
    value_side = split_proj[:, :, 2]
    key_index = jnp.arange(L, dtype=jnp.int32)
    valid_keys = (key_index[None, :] < group_lengths[:, None])[:, None, None, :]
    raw_scores = jnp.einsum('gqhd,gkhd->ghqk', query_side, key_side) * scale_factor
    scores = jnp.where(valid_keys, raw_scores, masked_score)
    row_top = lax.optimization_barrier(jnp.max(scores, axis=-1, keepdims=True))
    log_total = row_top + jnp.log(lax.optimization_barrier(jnp.sum(jnp.exp(scores - row_top), axis=-1, keepdims=True)))
    probs = jnp.exp(scores - log_total)
    probs_low = rounded(probs)
    context = jnp.einsum('ghqk,gkhd->gqhd', probs_low, value_side)
    context_low = context.astype(jnp.bfloat16).reshape(row_count, D)
    first_sum = flat_tokens.astype(jnp.float32) + jnp.dot(context_low, out_weight, preferred_element_type=jnp.float32) + out_bias.astype(jnp.float32)
    normed_one, scale_one = normalize(first_sum)
    first_out = normed_one * norm1_gain.astype(jnp.float32) + norm1_bias.astype(jnp.float32)
    first_low = first_out.astype(jnp.bfloat16)
    pre_act = jnp.dot(first_low, up_weight, preferred_element_type=jnp.float32) + up_bias.astype(jnp.float32)
    act_value, act_slope = gelu_pair(pre_act)
    act_low = act_value.astype(jnp.bfloat16)
    second_sum = first_out + jnp.dot(act_low, down_weight, preferred_element_type=jnp.float32) + down_bias.astype(jnp.float32)
    normed_two, scale_two = normalize(second_sum)
    hidden_out = (normed_two * norm2_gain.astype(jnp.float32) + norm2_bias.astype(jnp.float32)).astype(jnp.bfloat16)
    grad_top = group_cot.reshape(row_count, D).astype(jnp.float32)
    gaintwo_grad = lax.optimization_barrier(jnp.sum(grad_top * normed_two, axis=0))
    biastwo_grad = lax.optimization_barrier(jnp.sum(grad_top, axis=0))
    second_grad = norm_back(grad_top * norm2_gain.astype(jnp.float32), normed_two, scale_two)
    second_low = second_grad.astype(jnp.bfloat16)
    downmat_grad = jnp.dot(act_low.T, second_low, preferred_element_type=jnp.float32)
    downvec_grad = lax.optimization_barrier(jnp.sum(second_grad, axis=0))
    pre_grad = jnp.dot(second_low, down_weight.T, preferred_element_type=jnp.float32) * act_slope
    pre_low = pre_grad.astype(jnp.bfloat16)
    upmat_grad = jnp.dot(first_low.T, pre_low, preferred_element_type=jnp.float32)
    upvec_grad = lax.optimization_barrier(jnp.sum(pre_grad, axis=0))
    first_out_grad = second_grad + jnp.dot(pre_low, up_weight.T, preferred_element_type=jnp.float32)
    gainone_grad = lax.optimization_barrier(jnp.sum(first_out_grad * normed_one, axis=0))
    biasone_grad = lax.optimization_barrier(jnp.sum(first_out_grad, axis=0))
    first_grad = norm_back(first_out_grad * norm1_gain.astype(jnp.float32), normed_one, scale_one)
    first_grad_low = first_grad.astype(jnp.bfloat16)
    outmat_grad = jnp.dot(context_low.T, first_grad_low, preferred_element_type=jnp.float32)
    outvec_grad = lax.optimization_barrier(jnp.sum(first_grad, axis=0))
    context_grad = rounded(jnp.dot(first_grad_low, out_weight.T, preferred_element_type=jnp.float32)).reshape(group_size, L, HEADS, HEAD_DIM)
    prob_grad = jnp.einsum('gqhd,gkhd->ghqk', context_grad, value_side)
    value_grad = jnp.einsum('ghqk,gqhd->gkhd', probs_low, context_grad).astype(jnp.bfloat16)
    score_grad = rounded(probs * (prob_grad - lax.optimization_barrier(jnp.sum(probs * prob_grad, axis=-1, keepdims=True))) * scale_factor)
    query_grad = jnp.einsum('ghqk,gkhd->gqhd', score_grad, key_side).astype(jnp.bfloat16)
    key_grad = jnp.einsum('ghqk,gqhd->gkhd', score_grad, query_side).astype(jnp.bfloat16)
    proj_grad_act = jnp.stack([query_grad, key_grad, value_grad], axis=2).reshape(row_count, 3 * D)
    proj_grad = jnp.dot(flat_tokens.T, proj_grad_act, preferred_element_type=jnp.float32)
    column_sums = lax.optimization_barrier(jnp.sum(proj_grad_act.astype(jnp.float32), axis=0))
    qvbias_grad = jnp.concatenate([column_sums[:D], column_sums[2 * D:]])
    tokens_grad = first_grad + jnp.dot(proj_grad_act, proj_weight.T, preferred_element_type=jnp.float32)
    grads = (proj_grad, qvbias_grad, outmat_grad, outvec_grad, gainone_grad, biasone_grad, upmat_grad, upvec_grad, downmat_grad, downvec_grad, gaintwo_grad, biastwo_grad)
    return (hidden_out.reshape(group_size, L, D), tokens_grad.reshape(group_size, L, D), grads)

def reference(tokens, lengths, cotangent, proj_weight, qv_bias, out_weight, out_bias, norm1_gain, norm1_bias, up_weight, up_bias, down_weight, down_bias, norm2_gain, norm2_bias):
    params = (proj_weight, qv_bias, out_weight, out_bias, norm1_gain, norm1_bias, up_weight, up_bias, down_weight, down_bias, norm2_gain, norm2_bias)
    group_size = math.gcd(SEQS, 8)
    group_count = SEQS // group_size

    def scan_step(carried, inputs):
        hidden_part, grad_part, grads = layer_group(params, inputs[0], inputs[1], inputs[2])
        return (tuple((total + extra for total, extra in zip(carried, grads))), (hidden_part, grad_part))
    initial = tuple((jnp.zeros(value.shape, jnp.float32) for value in params))
    grouped = (tokens.reshape(group_count, group_size, L, D), cotangent.reshape(group_count, group_size, L, D), lengths.reshape(group_count, group_size))
    totals, stacked = lax.scan(scan_step, initial, grouped)
    proj_grad, qvbias_grad, outmat_grad, outvec_grad, gainone_grad, biasone_grad, upmat_grad, upvec_grad, downmat_grad, downvec_grad, gaintwo_grad, biastwo_grad = totals
    hidden_out = stacked[0].reshape(SEQS, L, D)
    tokens_grad = stacked[1].reshape(SEQS, L, D)
    return (hidden_out, tokens_grad, proj_grad, qvbias_grad, outmat_grad, outvec_grad, gainone_grad, biasone_grad, upmat_grad, upvec_grad, downmat_grad, downvec_grad, gaintwo_grad, biastwo_grad)
```

```python
import functools
import math

import jax
import jax.numpy as jnp
from jax import lax
from jax.experimental import pallas as pl
from jax.experimental.pallas import tpu as pltpu
from jax.sharding import PartitionSpec as P

HEADS = 12
HEAD_DIM = 64
epsilon = 1e-05
masked_score = -1e30
bf16 = jnp.bfloat16
f32 = jnp.float32


NT = (((1,), (1,)), ((), ()))
TN = (((0,), (0,)), ((), ()))


def normalize(rows):
    centred = rows - jnp.mean(rows, axis=-1, keepdims=True)
    inv_scale = lax.rsqrt(jnp.mean(centred * centred, axis=-1, keepdims=True) + epsilon)
    return (centred * inv_scale, inv_scale)


def norm_back(grad_norm, normed, inv_scale):
    first_mean = jnp.mean(grad_norm, axis=-1, keepdims=True)
    second_mean = jnp.mean(grad_norm * normed, axis=-1, keepdims=True)
    return inv_scale * (grad_norm - first_mean - normed * second_mean)


def gelu_pair(pre_act):
    cumulative = 0.5 * (1.0 + jax.scipy.special.erf(pre_act * (1.0 / math.sqrt(2.0))))
    density = jnp.exp(-0.5 * pre_act * pre_act) * (1.0 / math.sqrt(2.0 * math.pi))
    return (pre_act * cumulative, cumulative + pre_act * density)


def valid_keys(who, length, count, rows):
    spot = lax.broadcasted_iota(jnp.int32, (1, count), 1)
    place = (who ^ (spot // rows)) * rows + spot % rows
    return place < length


def attention_forward(parts, seq_dev, scal, *refs):
    toks = refs[: seq_dev * parts]
    weight, bias = refs[seq_dev * parts : seq_dev * parts + 2]
    outs = refs[seq_dev * parts + 2 :]
    qkv_out, log_out = outs[0], outs[1]
    ctx_out = outs[2:]
    rows = toks[0].shape[0]
    count = rows * parts
    wide = weight.shape[1] // 3
    scale = 1.0 / math.sqrt(HEAD_DIM)
    for q in range(seq_dev):
        x = jnp.concatenate([toks[q * parts + j][...] for j in range(parts)], axis=0)
        qkv = jnp.dot(x, weight[...], preferred_element_type=f32) + bias[...]
        qkv = qkv.astype(bf16)
        qkv_out[q] = qkv
        valid = valid_keys(scal[0], scal[1 + q], count, rows)
        lane = lax.broadcasted_iota(jnp.int32, (count, 128), 1)
        logs = jnp.zeros((count, 128), f32)
        heads = []
        for h in range(wide // HEAD_DIM):
            lo = h * HEAD_DIM
            query = qkv[:, lo : lo + HEAD_DIM]
            key = qkv[:, wide + lo : wide + lo + HEAD_DIM]
            value = qkv[:, 2 * wide + lo : 2 * wide + lo + HEAD_DIM]
            scores = lax.dot_general(query, key, NT, preferred_element_type=f32) * scale
            scores = jnp.where(valid, scores, masked_score)
            top = jnp.max(scores, axis=-1, keepdims=True)
            raised = jnp.exp(scores - top)
            total = jnp.sum(raised, axis=-1, keepdims=True)
            probs = (raised * (1.0 / total)).astype(bf16)
            heads.append(jnp.dot(probs, value, preferred_element_type=f32).astype(bf16))
            logs = jnp.where(lane == h, top + jnp.log(total), logs)
        ctx = jnp.concatenate(heads, axis=1)
        log_out[q] = logs
        for j in range(parts):
            ctx_out[j][q] = ctx[j * rows : (j + 1) * rows]


def attention_backward(parts, seq_dev, scal, *refs):
    n = seq_dev * parts
    toks = refs[:n]
    qkv_in, log_in, weight = refs[n : n + 3]
    grads = refs[n + 3 : n + 3 + parts]
    outs = refs[n + 3 + parts :]
    tok_own = outs[0]
    tok_send = outs[1 : 1 + seq_dev * (parts - 1)]
    own_half, other_half, sums_out, whole = outs[1 + seq_dev * (parts - 1) :]
    rows = toks[0].shape[0]
    count = rows * parts
    wide = weight.shape[1] // 3
    scale = 1.0 / math.sqrt(HEAD_DIM)
    for q in range(seq_dev):
        x = jnp.concatenate([toks[q * parts + j][...] for j in range(parts)], axis=0)
        qkv = qkv_in[q]
        logs = log_in[q]
        ctx_grad = jnp.concatenate([grads[j][q] for j in range(parts)], axis=0)
        valid = valid_keys(scal[0], scal[1 + q], count, rows)
        dq, dk, dv = [], [], []
        for h in range(wide // HEAD_DIM):
            lo = h * HEAD_DIM
            query = qkv[:, lo : lo + HEAD_DIM]
            key = qkv[:, wide + lo : wide + lo + HEAD_DIM]
            value = qkv[:, 2 * wide + lo : 2 * wide + lo + HEAD_DIM]
            grad = ctx_grad[:, lo : lo + HEAD_DIM]
            scores = lax.dot_general(query, key, NT, preferred_element_type=f32) * scale
            scores = jnp.where(valid, scores, masked_score)
            probs = jnp.exp(scores - logs[:, h : h + 1])
            prob_grad = lax.dot_general(grad, value, NT, preferred_element_type=f32)
            dv.append(lax.dot_general(probs.astype(bf16), grad, TN, preferred_element_type=f32).astype(bf16))
            weighed = probs * prob_grad
            row_term = jnp.sum(weighed, axis=-1, keepdims=True)
            score_grad = ((weighed - probs * row_term) * scale).astype(bf16)
            dq.append(jnp.dot(score_grad, key, preferred_element_type=f32).astype(bf16))
            dk.append(lax.dot_general(score_grad, query, TN, preferred_element_type=f32).astype(bf16))
        act_grad = jnp.concatenate(dq + dk + dv, axis=1)
        tok_grad = lax.dot_general(act_grad, weight[...], NT, preferred_element_type=f32)
        tok_own[q] = tok_grad[:rows]
        for j in range(1, parts):
            tok_send[q * (parts - 1) + j - 1][...] = tok_grad[j * rows : (j + 1) * rows].astype(bf16)
        sums = jnp.sum(act_grad.astype(f32), axis=0, keepdims=True)
        part = lax.dot_general(x, act_grad, TN, preferred_element_type=f32)
        if q == 0:
            sums_out[...] = sums
            whole[...] = part
        else:
            sums_out[...] += sums
            whole[...] += part
    core = scal[1 + seq_dev]
    planes, piece = own_half.shape[0], own_half.shape[1]
    for p in range(planes):
        mine = pl.multiple_of((2 * p + core) * piece, 8)
        theirs = pl.multiple_of((2 * p + 1 - core) * piece, 8)
        own_half[p] = whole[pl.ds(mine, piece), :]
        other_half[p] = whole[pl.ds(theirs, piece), :].astype(bf16)


def solution(mesh):
    seq_size = mesh.shape["seq"]
    fsdp_size = mesh.shape["fsdp"]
    planes = fsdp_size // 2
    assert seq_size == 4 and fsdp_size % 2 == 0

    swap_x = [(i, i ^ 1) for i in range(seq_size)]
    swap_y = [(i, i ^ 2) for i in range(seq_size)]
    swap_xy = [(i, i ^ 3) for i in range(seq_size)]
    swap_core = [(i, i ^ 1) for i in range(fsdp_size)]

    def shift(d):
        return [(i, ((i // 2 + d) % planes) * 2 + i % 2) for i in range(fsdp_size)]

    def over_x(value):
        return lax.ppermute(value, "seq", swap_x)

    def over_y(value):
        return lax.ppermute(value, "seq", swap_y)

    def over_xy(value):
        return lax.ppermute(value, "seq", swap_xy)

    def over_core(value):
        return lax.ppermute(value, "fsdp", swap_core)

    def per_device(
        tokens,
        lengths,
        cotangent,
        proj_weight,
        qv_bias,
        out_weight,
        out_bias,
        norm1_gain,
        norm1_bias,
        up_weight,
        up_bias,
        down_weight,
        down_bias,
        norm2_gain,
        norm2_bias,
    ):
        seq_dev, rows, dim = tokens.shape
        hidden = up_weight.shape[1]
        local = dim // fsdp_size
        unit = hidden // fsdp_size // seq_size
        slab = fsdp_size * unit
        wide = dim // seq_size
        sliver = local // seq_size
        s = lax.axis_index("seq")
        f = lax.axis_index("fsdp")
        z, c = f // 2, f % 2
        xbit, ybit = (s & 1) == 1, (s & 2) == 2

        def natural_planes(parts):
            cur = [parts[(-k) % planes] for k in range(planes)]
            step = 1
            while step < planes:
                cur = [jnp.where((z & step) != 0, cur[(k - step) % planes], cur[k]) for k in range(planes)]
                step *= 2
            return jnp.stack(cur)

        def natural_seq(parts):
            cur = [jnp.where(xbit, parts[k ^ 1], parts[k]) for k in range(4)]
            return [jnp.where(ybit, cur[k ^ 2], cur[k]) for k in range(4)]

        def plane_gather(value):
            return natural_planes([value] + [lax.ppermute(value, "fsdp", shift(d)) for d in range(1, planes)])

        def core_pair(mine, other, axis):
            return jnp.where(
                c == 0, jnp.stack([mine, other], axis=axis), jnp.stack([other, mine], axis=axis)
            )

        def core_gather(value, axis=1):
            return core_pair(value, over_core(value), axis)

        def x_first_gather(value):
            one, two = over_x(value), over_y(value)
            return [value, one, two, over_y(one)]

        def y_first_gather(value):
            two, one = over_y(value), over_x(value)
            return [value, one, two, over_x(two)]

        def add(*terms):
            total = terms[0].astype(f32)
            for term in terms[1:]:
                total = total + term.astype(f32)
            return total

        def y_first_reduce(blocks):
            two, three = over_y(blocks[2]), over_y(blocks[3])
            one = over_x(add(blocks[1], three).astype(bf16))
            return add(blocks[0], two, one)

        def x_first_reduce(blocks):
            one, three = over_x(blocks[1]), over_x(blocks[3])
            two = over_y(add(blocks[2], three).astype(bf16))
            return add(blocks[0], one, two)

        def plane_reduce(stacked):
            low = stacked.astype(bf16)
            total = lax.dynamic_index_in_dim(stacked, z, 0, keepdims=False).astype(f32)
            for d in range(1, planes):
                piece = lax.dynamic_index_in_dim(low, (z + d) % planes, 0, keepdims=False)
                total = total + lax.ppermute(piece, "fsdp", shift(d)).astype(f32)
            return total

        token_blocks = []
        for q in range(seq_dev):
            gather = x_first_gather if q % 2 == 0 else y_first_gather
            token_blocks.append(gather(tokens[q]))

        small_list = [qv_bias, out_bias, norm1_gain, norm1_bias, up_bias, down_bias, norm2_gain, norm2_bias]
        small_sizes = [v.shape[0] for v in small_list]
        small = jnp.concatenate(small_list)
        third = 3 * wide
        small_rows = -(-small.shape[0] // third)
        small_rows = -(-small_rows // 8) * 8
        small = jnp.pad(small, (0, small_rows * third - small.shape[0])).reshape(small_rows, third)
        proj_own = lax.dynamic_index_in_dim(
            proj_weight.reshape(local, 3, seq_size, wide), s, 2, keepdims=False
        ).reshape(local, third)
        first_pack = jnp.concatenate([proj_own, small], axis=0)
        first_planes = plane_gather(first_pack)
        first_whole = core_gather(first_planes)
        proj_cols = first_whole[:, :, :local].reshape(dim, third)
        small_whole = first_whole[:, :, local:].reshape(fsdp_size, small_rows * third)
        small_out, offset = [], 0
        for size in small_sizes:
            small_out.append(small_whole[:, offset : offset + size].reshape(-1).astype(f32))
            offset += size
        qv_float, outvec, gainone, biasone, upvec, downvec, gaintwo, biastwo = small_out
        qv_own = lax.dynamic_index_in_dim(qv_float.reshape(2, seq_size, wide), s, 1, keepdims=False)
        bias_own = jnp.concatenate([qv_own[0], jnp.zeros((wide,), f32), qv_own[1]])[None, :]

        up_own = lax.dynamic_index_in_dim(
            up_weight.reshape(local, fsdp_size, seq_size, unit), s, 2, keepdims=False
        ).reshape(local, slab)
        down_own = lax.dynamic_index_in_dim(
            down_weight.reshape(seq_size, unit, dim), s, 0, keepdims=False
        )
        out_own = lax.dynamic_index_in_dim(
            out_weight.reshape(seq_size, sliver, dim), s, 0, keepdims=False
        )
        up_planes = plane_gather(jnp.concatenate([up_own, out_own], axis=0))
        down_planes = plane_gather(down_own)
        up_quarters = [core_gather(v) for v in x_first_gather(up_planes)]
        down_quarters = [core_gather(v) for v in y_first_gather(down_planes)]
        upmat = jnp.concatenate([v[:, :, :local].reshape(dim, slab) for v in up_quarters], axis=1)
        outmat = jnp.stack(natural_seq([v[:, :, local:] for v in up_quarters]), axis=2).reshape(dim, dim)
        downmat = jnp.concatenate([v.reshape(slab, dim) for v in down_quarters], axis=0)
        up_parts = natural_seq([upvec.reshape(fsdp_size, seq_size, unit)[:, k].reshape(slab) for k in range(4)])
        upvec_blocks = jnp.concatenate(up_parts)

        scal = jnp.concatenate([s[None], lengths, c[None]]).astype(jnp.int32)
        smem = pl.BlockSpec(memory_space=pltpu.SMEM)
        vmem = pl.BlockSpec(memory_space=pltpu.VMEM)
        flat_tokens = [b for blocks in token_blocks for b in blocks]
        count = rows * seq_size
        heads_here = wide // HEAD_DIM
        square = seq_dev * heads_here * count * count
        proj_flops = 2 * seq_dev * count * dim * third
        forward = pl.pallas_call(
            functools.partial(attention_forward, seq_size, seq_dev),
            out_shape=[
                jax.ShapeDtypeStruct((seq_dev, count, third), bf16),
                jax.ShapeDtypeStruct((seq_dev, count, 128), f32),
            ]
            + [jax.ShapeDtypeStruct((seq_dev, rows, wide), bf16)] * seq_size,
            in_specs=[smem] + [vmem] * (len(flat_tokens) + 2),
            out_specs=[vmem] * (2 + seq_size),
            cost_estimate=pl.CostEstimate(
                flops=proj_flops + 4 * square * HEAD_DIM * 2,
                bytes_accessed=6_000_000,
                transcendentals=square,
            ),
            name="attention_forward",
        )
        qkv, log_total, *ctx_send = forward(scal, *flat_tokens, proj_cols, bias_own)
        ctx_blocks = [ctx_send[0], over_x(ctx_send[1]), over_y(ctx_send[2]), over_xy(ctx_send[3])]
        context = jnp.concatenate(natural_seq(ctx_blocks), axis=2).reshape(seq_dev * rows, dim)

        flat = tokens.reshape(seq_dev * rows, dim).astype(f32)
        first_sum = flat + jnp.dot(context, outmat, preferred_element_type=f32) + outvec
        normed_one, scale_one = normalize(first_sum)
        first_out = normed_one * gainone + biasone
        first_low = first_out.astype(bf16)
        pre_act = jnp.dot(first_low, upmat, preferred_element_type=f32) + upvec_blocks
        act_value, act_slope = gelu_pair(pre_act)
        act_low = act_value.astype(bf16)
        second_sum = first_out + jnp.dot(act_low, downmat, preferred_element_type=f32) + downvec
        normed_two, scale_two = normalize(second_sum)
        hidden_out = (normed_two * gaintwo + biastwo).astype(bf16).reshape(seq_dev, rows, dim)

        grad_top = cotangent.reshape(seq_dev * rows, dim).astype(f32)
        gaintwo_grad = jnp.sum(grad_top * normed_two, axis=0)
        biastwo_grad = jnp.sum(grad_top, axis=0)
        second_grad = norm_back(grad_top * gaintwo, normed_two, scale_two)
        second_low = second_grad.astype(bf16)

        def halves(stacked, axis):
            mine = lax.dynamic_index_in_dim(stacked, c, axis, keepdims=False)
            other = lax.dynamic_index_in_dim(stacked, 1 - c, axis, keepdims=False)
            return add(mine, over_core(other)).astype(bf16)

        downmat_grad = lax.dot_general(act_low, second_low, TN, preferred_element_type=f32).astype(bf16)
        down_half = halves(downmat_grad.reshape(seq_size, planes, 2, unit, dim), 2)
        down_sum = x_first_reduce([down_half[j] for j in range(4)])

        downvec_grad = jnp.sum(second_grad, axis=0)
        pre_grad = lax.dot_general(second_low, downmat, NT, preferred_element_type=f32) * act_slope
        pre_low = pre_grad.astype(bf16)
        upmat_grad = lax.dot_general(first_low, pre_low, TN, preferred_element_type=f32).astype(bf16)
        up_half = halves(upmat_grad.reshape(planes, 2, local, hidden), 1)
        up_sum = y_first_reduce([up_half[:, :, j * slab : (j + 1) * slab] for j in range(4)])

        upvec_grad = jnp.sum(pre_grad, axis=0).reshape(4, fsdp_size, unit)
        first_out_grad = second_grad + lax.dot_general(pre_low, upmat, NT, preferred_element_type=f32)
        gainone_grad = jnp.sum(first_out_grad * normed_one, axis=0)
        biasone_grad = jnp.sum(first_out_grad, axis=0)
        first_grad = norm_back(first_out_grad * gainone, normed_one, scale_one)
        first_grad_low = first_grad.astype(bf16)
        context_grad = lax.dot_general(first_grad_low, outmat, NT, preferred_element_type=f32)
        context_grad = context_grad.astype(bf16).reshape(seq_dev, rows, seq_size, wide)
        grad_send = natural_seq([context_grad[:, :, k] for k in range(4)])
        ctx_grads = [grad_send[0], over_x(grad_send[1]), over_y(grad_send[2]), over_xy(grad_send[3])]

        outmat_grad = lax.dot_general(context, first_grad_low, TN, preferred_element_type=f32).astype(bf16)
        outvec_grad = jnp.sum(first_grad, axis=0)
        out_half = halves(outmat_grad.reshape(planes, 2, seq_size, sliver, dim), 1)
        out_sum = y_first_reduce(natural_seq([out_half[:, k] for k in range(4)]))

        upvec_natural = jnp.stack(natural_seq([upvec_grad[j] for j in range(4)]), axis=1)
        small_grads = jnp.concatenate(
            [v.reshape(fsdp_size, -1) for v in (outvec_grad, gainone_grad, biasone_grad)]
            + [upvec_natural.reshape(fsdp_size, -1)]
            + [v.reshape(fsdp_size, -1) for v in (downvec_grad, gaintwo_grad, biastwo_grad)],
            axis=1,
        )
        small_grads = small_grads + over_x(small_grads)
        small_grads = small_grads + over_y(small_grads)
        small_grads = small_grads.reshape(planes, 2, -1)
        small_mine = lax.dynamic_index_in_dim(small_grads, c, 1, keepdims=False)
        small_other = lax.dynamic_index_in_dim(small_grads, 1 - c, 1, keepdims=False)
        small_pair = small_mine + over_core(small_other)
        small_total = lax.dynamic_index_in_dim(small_pair, z, 0, keepdims=False)
        for d in range(1, planes):
            piece = lax.dynamic_index_in_dim(small_pair, (z + d) % planes, 0, keepdims=False)
            small_total = small_total + lax.ppermute(piece[None], "fsdp", shift(d))[0]

        backward = pl.pallas_call(
            functools.partial(attention_backward, seq_size, seq_dev),
            out_shape=[jax.ShapeDtypeStruct((seq_dev, rows, dim), f32)]
            + [jax.ShapeDtypeStruct((rows, dim), bf16)] * (seq_dev * (seq_size - 1))
            + [
                jax.ShapeDtypeStruct((planes, local, third), f32),
                jax.ShapeDtypeStruct((planes, local, third), bf16),
                jax.ShapeDtypeStruct((1, third), f32),
            ],
            in_specs=[smem] + [vmem] * (len(flat_tokens) + 3 + seq_size),
            out_specs=[vmem] * (1 + seq_dev * (seq_size - 1) + 3),
            scratch_shapes=[pltpu.VMEM((dim, third), f32)],
            cost_estimate=pl.CostEstimate(
                flops=2 * proj_flops + 10 * square * HEAD_DIM * 2,
                bytes_accessed=10_000_000,
                transcendentals=square,
            ),
            name="attention_backward",
        )
        results = backward(scal, *flat_tokens, qkv, log_total, proj_cols, *ctx_grads)
        tok_own = results[0]
        tok_send = results[1 : 1 + seq_dev * (seq_size - 1)]
        proj_mine, proj_other, col_sums = results[1 + seq_dev * (seq_size - 1) :]

        tok_total = []
        for q in range(seq_dev):
            blocks = [tok_own[q]] + list(tok_send[q * 3 : q * 3 + 3])
            reduce = y_first_reduce if q % 2 == 0 else x_first_reduce
            tok_total.append(reduce(blocks))
        tokens_grad = first_grad.reshape(seq_dev, rows, dim) + jnp.stack(tok_total)

        sums_high = col_sums.astype(bf16)
        sums_low = (col_sums - sums_high.astype(f32)).astype(bf16)
        extra = jnp.concatenate([sums_high, sums_low, jnp.zeros((6, third), bf16)], axis=0)
        extra = jnp.broadcast_to(extra[None], (planes, 8, third))
        other_pack = jnp.concatenate([proj_other, extra], axis=1)
        mine_pack = jnp.concatenate([proj_mine, extra.astype(f32)], axis=1)
        proj_pair = add(mine_pack, over_core(other_pack))
        pair_sums = proj_pair[0, local] + proj_pair[0, local + 1]
        pair_high = pair_sums.astype(bf16)
        pair_low = (pair_sums - pair_high.astype(f32)).astype(bf16)
        pair_extra = jnp.concatenate([pair_high[None], pair_low[None], jnp.zeros((6, third), bf16)], axis=0)
        pair_extra = jnp.broadcast_to(pair_extra[None].astype(f32), (planes, 8, third))
        proj_total = plane_reduce(jnp.concatenate([proj_pair[:, :local], pair_extra], axis=1))
        all_sums = proj_total[local] + proj_total[local + 1]
        sums_high = all_sums.astype(bf16)
        sums_low = (all_sums - sums_high.astype(f32)).astype(bf16)
        last_pack = jnp.concatenate(
            [proj_total[:local].astype(bf16), sums_high[None], sums_low[None], jnp.zeros((6, third), bf16)], axis=0
        )
        last_blocks = natural_seq([last_pack, over_x(last_pack), over_y(last_pack), over_xy(last_pack)])
        proj_part = jnp.stack([b[:local].reshape(local, 3, wide) for b in last_blocks], axis=2)
        proj_part = proj_part.reshape(local, 3 * dim).astype(f32)
        sum_blocks = [
            (b[local].astype(f32) + b[local + 1].astype(f32)).reshape(3, wide) for b in last_blocks
        ]
        qv_all = jnp.concatenate([b[0] for b in sum_blocks] + [b[2] for b in sum_blocks])
        qvbias_part = lax.dynamic_slice(qv_all, (f * qv_bias.shape[0],), (qv_bias.shape[0],))

        owned = plane_reduce(jnp.concatenate([up_sum, down_sum, out_sum], axis=1)).astype(bf16)
        owned_blocks = natural_seq([owned, over_x(owned), over_y(owned), over_xy(owned)])
        upmat_part = jnp.stack(
            [b[:local].reshape(local, fsdp_size, unit) for b in owned_blocks], axis=2
        ).reshape(local, hidden).astype(f32)
        downmat_part = jnp.concatenate([b[local : local + unit] for b in owned_blocks], axis=0).astype(f32)
        outmat_part = jnp.concatenate([b[local + unit :] for b in owned_blocks], axis=0).astype(f32)

        sizes = small_sizes[1:]
        parts, offset = [], 0
        for size in sizes:
            parts.append(small_total[offset : offset + size])
            offset += size
        outvec_part, gainone_part, biasone_part, upvec_part, downvec_part, gaintwo_part, biastwo_part = parts
        return (
            hidden_out,
            tokens_grad,
            proj_part,
            qvbias_part,
            outmat_part,
            outvec_part,
            gainone_part,
            biasone_part,
            upmat_part,
            upvec_part,
            downmat_part,
            downvec_part,
            gaintwo_part,
            biastwo_part,
        )

    block = P("fsdp", "seq", None)
    matrix = P("fsdp", None)
    vector = P("fsdp")
    in_specs = (
        block,
        vector,
        block,
        matrix,
        vector,
        matrix,
        vector,
        vector,
        vector,
        matrix,
        vector,
        matrix,
        vector,
        vector,
        vector,
    )
    out_specs = (
        block,
        block,
        matrix,
        vector,
        matrix,
        vector,
        vector,
        vector,
        matrix,
        vector,
        matrix,
        vector,
        vector,
        vector,
    )
    return jax.shard_map(
        per_device, mesh=mesh, in_specs=in_specs, out_specs=out_specs, check_vma=False
    )
```
